512 devices in a mesh: rep: 2 (over x_lo), dp: 32 (over z, core), tensor: 8 (over x_hi, y).
Axes of the slice: x: 4 (x_hi: 2, x_lo: 2; x = x_hi * 2 + x_lo), y: 4, z: 16, core: 2. Of those that a mesh axis runs over, the one named last changes fastest.
Arguments:
- tokens: bfloat16 [64, 1024, 1536], P(('rep', 'dp'), 'tensor'), may hold values from -6 to 6
- norm_gain: float32 [1536], replicated, may hold values from 0.25 to 1.75
- w_query: bfloat16 [1536, 1536], P(None, 'tensor'), may hold values from -0.15625 to 0.15625
- w_keyval: bfloat16 [1536, 512], replicated, may hold values from -0.15625 to 0.15625
- w_out: bfloat16 [1536, 1536], P('tensor'), may hold values from -0.15625 to 0.15625
- kv_pages: bfloat16 [512, 128, 512], P(('rep', 'dp'), 'tensor')
- page_table: int32 [64, 8], P(('rep', 'dp')), may hold values from 0 to 511, as said below
- lengths: int32 [64], P(('rep', 'dp')), may hold values from 1 to 1024, as said below
- starts: int32 [64], P(('rep', 'dp')), may hold values from 1024 to 3968, as said below
Outputs:
- attended: bfloat16 [64, 1024, 1536], P(('rep', 'dp'), 'tensor')
The draws below stay inside these ranges and needn't reach their ends.
Inputs may be any that keep to these rules, and one draw needn't show every extreme that they name: `page_table`: all 8 pages of a group lie on one replica: its own, or the other one for some groups. Page q is held by the group q // 8 (counted over rep, then dp), whose dp index is within 3 of the group's own, cyclically. `lengths`: some group is full in every draw. `starts`: multiples of 128.
All inputs are finite; a program needn't handle non-finite values.
Results may differ from the reference program's by a relative error of at most 0.034.
Values may be sent and summed in bfloat16 or wider, within the bound.
A program may use at most 64 MiB of HBM per device.

```python
import math
import jax
import jax.numpy as jnp
from jax import lax

D = 1536
HEADS = 6
HD = 256
PAGE = 128
CTXP = 8
NEAR = 3
TOK = 1024
PPD = 8
WIN = 1024
GROUPS = 64
POOL = 512
N_TENSOR = 8


def draw_kv_pages(key, part):
    first = jax.random.fold_in(key, 0)
    base = jax.random.normal(first, (POOL, PAGE, 2 * HD), jnp.float32)
    return base.astype(jnp.bfloat16)


def draw_page_table(key, part):
    first, second, third = jax.random.split(key, 3)
    half = GROUPS // 2
    moved = (jax.random.randint(first, (GROUPS,), 0, 4) == 0).astype(jnp.int32)
    offset = jax.random.randint(second, (GROUPS, CTXP), -NEAR, NEAR + 1)
    slot = jax.random.randint(third, (GROUPS, CTXP), 0, PPD)
    group = jnp.arange(GROUPS, dtype=jnp.int32)
    home = group // half
    place = group % half
    side = (home + moved) % 2
    holder = side[:, None] * half + jnp.remainder(place[:, None] + offset, half)
    return (holder * PPD + slot).astype(jnp.int32)


def draw_lengths(key, part):
    first, second = jax.random.split(key)
    sizes = jax.random.randint(first, (GROUPS,), 1, TOK + 1)
    fullest = jax.random.randint(second, (), 0, GROUPS)
    return sizes.at[fullest].set(TOK).astype(jnp.int32)


def draw_starts(key, part):
    return (PAGE * jax.random.randint(key, (GROUPS,), CTXP, 4 * CTXP)).astype(jnp.int32)


def level_of(rng, shape, cuts, low, largest):
    def one(axis_at, shards_of):
        steps = jax.random.uniform(jax.random.fold_in(jax.random.fold_in(rng, 6), axis_at), (shards_of,), jnp.float32, low / len(cuts), largest / len(cuts))
        return jnp.repeat(jnp.exp(steps), shape[axis_at] // shards_of).reshape((-1,) + (1,) * (len(shape) - axis_at - 1))

    factor_of = one(*cuts[0])
    for cut in cuts[1:]:
        factor_of = factor_of * one(*cut)
    return factor_of


def centred(stream_key, dims, scale, most, cuts=(), held_as=jnp.bfloat16):
    array = jax.random.normal(stream_key, dims, jnp.float32) * scale
    if len(cuts) > 0:
        array = level_of(stream_key, dims, cuts, -0.22, 0.18) * array
    return jnp.clip(array, min=-most, max=most).astype(held_as)


def setup_inputs(seed: int = 0) -> dict:
    key_of = jax.random.split(jax.random.key(seed), 10)
    tokens = centred(key_of[0], (GROUPS, TOK, D), 1.0, 6.0, ((0, 64), (1, 8)))
    norm_gain = jnp.clip(1.0 + 0.15 * jax.random.normal(key_of[1], (D,), jnp.float32), 0.25, 1.75)
    w_query = centred(key_of[2], (D, D), D ** -0.5, 0.15625, ((1, 8),))
    w_keyval = centred(key_of[3], (D, 2 * HD), D ** -0.5, 0.15625)
    w_out = centred(key_of[4], (D, D), D ** -0.5, 0.15625, ((0, 8),))
    kv_pages = draw_kv_pages(jax.random.fold_in(key_of[9], 71), 0)
    page_table = draw_page_table(jax.random.fold_in(key_of[9], 71), 0)
    lengths = draw_lengths(jax.random.fold_in(key_of[9], 71), 0)
    starts = draw_starts(jax.random.fold_in(key_of[9], 71), 0)
    return dict(tokens=tokens, norm_gain=norm_gain, w_query=w_query, w_keyval=w_keyval, w_out=w_out, kv_pages=kv_pages, page_table=page_table, lengths=lengths, starts=starts)


def rotate_pairs(values, positions, columns_from, head_size):
    rows, cols = values.shape
    column = columns_from + jnp.arange(cols // 2, dtype=jnp.int32) * 2
    within = (column % head_size).astype(jnp.float32)
    inv_freq = jnp.exp(within * (-math.log(10000.0) / head_size))
    angle = positions[:, None] * inv_freq[None, :]
    cosine = jnp.cos(angle)
    sine = jnp.sin(angle)
    pairs = values.reshape(rows, cols // 2, 2)
    first = pairs[:, :, 0]
    second = pairs[:, :, 1]
    turned = jnp.stack([first * cosine - second * sine, first * sine + second * cosine], axis=-1)
    return turned.reshape(rows, cols)

def attend(query, keys, values, first_row):
    rows = query.shape[0]
    count = keys.shape[0]
    q_heads = query.reshape(rows, HEADS, HD).astype(jnp.float32)
    scores = jnp.einsum('rhd,kd->hrk', q_heads, keys.astype(jnp.float32)) * (1.0 / math.sqrt(HD))
    row_ids = first_row + jnp.arange(rows, dtype=jnp.int32)
    key_ids = jnp.arange(count, dtype=jnp.int32)
    seen = (key_ids[None, :] >= row_ids[:, None] + 1) & (key_ids[None, :] <= row_ids[:, None] + WIN)
    scores = jnp.where(seen[None, :, :], scores, -1e+30)
    top = lax.optimization_barrier(jnp.max(scores, axis=-1, keepdims=True))
    expd = jnp.exp(scores - top)
    total = lax.optimization_barrier(jnp.sum(expd, axis=-1, keepdims=True))
    probs = (expd / total).astype(jnp.bfloat16)
    mixed = jnp.einsum('hrk,kd->rhd', probs.astype(jnp.float32), values.astype(jnp.float32))
    return mixed.reshape(rows, HEADS * HD).astype(jnp.bfloat16)

def reference(tokens, norm_gain, w_query, w_keyval, w_out, kv_pages, page_table, lengths, starts):

    def one_group(packed):
        rows_in, table_row, length, start = packed
        xf = rows_in.astype(jnp.float32)
        scale = lax.rsqrt(lax.optimization_barrier(jnp.mean(xf * xf, axis=-1, keepdims=True)) + 1e-06)
        normed = (xf * scale * norm_gain).astype(jnp.bfloat16)
        positions = (start + jnp.arange(TOK, dtype=jnp.int32)).astype(jnp.float32)
        query = rotate_pairs(jnp.dot(normed, w_query, preferred_element_type=jnp.float32), positions, 0, HD).astype(jnp.bfloat16)
        keyval = jnp.dot(normed, w_keyval, preferred_element_type=jnp.float32)
        new_keys = rotate_pairs(keyval[:, :HD], positions, 0, HD).astype(jnp.bfloat16)
        new_values = keyval[:, HD:].astype(jnp.bfloat16)
        cached = kv_pages[table_row].reshape(WIN, 2 * HD)
        keys = jnp.concatenate([cached[:, :HD], new_keys], axis=0)
        values = jnp.concatenate([cached[:, HD:], new_values], axis=0)
        mixed = attend(query, keys, values, 0)
        blocks = mixed.reshape(TOK, N_TENSOR, D // N_TENSOR).astype(jnp.float32)
        weight_blocks = w_out.reshape(N_TENSOR, D // N_TENSOR, D).astype(jnp.float32)
        partial_value = jnp.einsum('tnc,ncd->ntd', blocks, weight_blocks)
        rounded = lax.optimization_barrier(partial_value.astype(jnp.bfloat16))
        summed = lax.optimization_barrier(jnp.sum(rounded.astype(jnp.float32), axis=0))
        live = jnp.arange(TOK, dtype=jnp.int32) < length
        return jnp.where(live[:, None], summed, 0.0).astype(jnp.bfloat16)
    return lax.map(one_group, (tokens, page_table, lengths, starts))
```

```python
import functools
import math

import jax
import jax.numpy as jnp
from jax import lax
from jax.experimental import pallas as pl
from jax.experimental.pallas import tpu as pltpu
from jax.sharding import PartitionSpec as P

MESH = pl.DeviceIdType.MESH
BF16 = jnp.bfloat16
F32 = jnp.float32
NT = (((1,), (1,)), ((), ()))


def fused(
    page_table, lengths, starts, tokens, gain, w_query, w_keyval, w_out, kv_pages,
    out,
    tok_v, normed, wraw, wkv, wq, wo, near_pages, mine, theirs, swapped, slots, window,
    cos_v, sin_v, query, mixed, acc, table_out, table_in, table_s,
    local_sem, w_send, w_direct, w_z, w_core, page_send, page_recv, swap_send, swap_recv,
    table_sem, slot_send, slot_recv, key_send, key_recv,
):
    rep = lax.axis_index("rep")
    dp = lax.axis_index("dp")
    ten = lax.axis_index("tensor")
    core = dp % 2
    par = (dp // 2) % 2
    xh = ten // 4
    y = ten % 4
    n_dp = 32

    def dev(r, d, t):
        return {"rep": r, "dp": d, "tensor": t}

    def near(k):
        return xh * 4 + (y + k) % 4

    def far(k):
        return (1 - xh) * 4 + (y + k) % 4

    y1, y3, y2 = (dev(rep, dp, near(k)) for k in (1, 3, 2))
    cross = dev(1 - rep, dp, far(0))
    twin = dev(1 - rep, dp, ten)
    sibling = dev(rep, dp + 1 - 2 * core, ten)
    z_up = dev(rep, (dp + 2) % n_dp, ten)
    z_down = dev(rep, (dp + n_dp - 2) % n_dp, ten)

    sends = []

    def push(src, dst, send, recv, to):
        copy = pltpu.make_async_remote_copy(
            src_ref=src, dst_ref=dst, send_sem=send, recv_sem=recv, device_id=to, device_id_type=MESH
        )
        copy.start()
        return copy

    def arrive(dst, recv, send):
        pltpu.make_async_remote_copy(
            src_ref=dst, dst_ref=dst, send_sem=send, recv_sem=recv, device_id=sibling, device_id_type=MESH
        ).wait_recv()

    def fetch(src, dst, k):
        copy = pltpu.make_async_copy(src, dst, local_sem.at[k])
        copy.start()
        return copy

    got_raw = fetch(w_query, wraw, 0)
    got_tok = fetch(tokens.at[0], tok_v, 1)
    got_wkv = fetch(w_keyval, wkv, 2)
    got_wo = fetch(w_out, wo.at[pl.ds(pl.multiple_of(ten * 192, 64), 192)], 3)
    got_pages = fetch(kv_pages, near_pages.at[pl.ds(24, 8)], 4)

    barrier = pltpu.get_barrier_semaphore()
    peers = [dev(rep, dp, (ten + k) % 8) for k in range(1, 8)]
    peers += [cross, twin]
    peers += [dev(rep, (dp + n_dp + k) % n_dp, ten) for k in (-3, -2, -1, 1, 2, 3)]
    for peer in peers:
        pl.semaphore_signal(barrier, inc=1, device_id=peer, device_id_type=MESH)

    lane = lax.broadcasted_iota(jnp.int32, (8, 128), 1)
    table = jnp.zeros((8, 128), jnp.int32)
    for j in range(8):
        table = jnp.where(lane == j, page_table[0, j], table)
    table_out[...] = table

    got_raw.wait()
    eye = (
        lax.broadcasted_iota(jnp.int32, (192, 192), 0) == lax.broadcasted_iota(jnp.int32, (192, 192), 1)
    ).astype(BF16)
    own_rows = pl.ds(pl.multiple_of(ten * 192, 64), 192)
    wq[own_rows, :] = lax.dot_general(eye, wraw[...], NT, preferred_element_type=F32).astype(BF16)
    got_wo.wait()

    pl.semaphore_wait(barrier, len(peers))

    page_copies = []
    for i, k in enumerate((-3, -2, -1, 1, 2, 3)):
        to = dev(rep, (dp + n_dp + k) % n_dp, ten)
        page_copies.append(
            push(kv_pages, near_pages.at[pl.ds((3 - k) * 8, 8)], page_send.at[i], page_recv.at[3 - k], to)
        )
    table_copy = push(table_out, table_in, table_sem.at[0], table_sem.at[1], twin)

    foreign = [near(1), near(3), far(0), near(2), far(1), far(3), far(2)]
    mats = (wq, wo)
    quarter = par * 2 + core

    def piece(m, s, q):
        return mats[m].at[pl.ds(pl.multiple_of(s * 192 + q * 48, 16), 48), :]

    def half(m, s, q, h):
        return mats[m].at[pl.ds(pl.multiple_of(s * 192 + q * 48, 16), 48), pl.ds(h * 768, 768)]

    def open_(m):
        for i, (to, q) in enumerate(
            ((y1, quarter), (y3, quarter), (cross, quarter), (y2, quarter))
        ):
            ref = piece(m, ten, q)
            sends.append(push(ref, ref, w_send.at[m, i], w_direct.at[m, ten], to))

    def relay(m, i):
        s = foreign[i]
        ref = piece(m, s, quarter)
        arrive(ref, w_direct.at[m, s], w_send.at[m, 0])
        if i in (0, 1):
            sends.append(push(ref, ref, w_send.at[m, 4 + i], w_direct.at[m, s], cross))
        if i == 2:
            sends.append(push(ref, ref, w_send.at[m, 6], w_direct.at[m, s], y2))
        for h, to in ((0, z_up), (1, z_down)):
            part = half(m, s, quarter, h)
            sends.append(push(part, part, w_send.at[m, 7 + 2 * i + h], w_z.at[m, s, h], to))
        sends.append(push(ref, ref, w_send.at[m, 21 + i], w_core.at[m, s, par], sibling))

    def across(m, i):
        s = foreign[i]
        q = (1 - par) * 2 + core
        for h in (0, 1):
            arrive(half(m, s, q, h), w_z.at[m, s, h], w_send.at[m, 0])
        ref = piece(m, s, q)
        sends.append(push(ref, ref, w_send.at[m, 28 + i], w_core.at[m, s, 1 - par], sibling))

    def settle(m, i):
        s = foreign[i]
        for k in (0, 1):
            arrive(piece(m, s, k * 2 + 1 - core), w_core.at[m, s, k], w_send.at[m, 0])

    open_(0)

    got_tok.wait()
    x = tok_v[...].astype(F32)
    scale = lax.rsqrt(jnp.mean(x * x, axis=-1, keepdims=True) + 1e-06)
    normed[...] = (x * scale * gain[...]).astype(BF16)
    row = lax.broadcasted_iota(jnp.int32, (128, 256), 0)
    col = lax.broadcasted_iota(jnp.int32, (128, 256), 1)
    even = col % 2 == 0
    inv_freq = jnp.exp((col - col % 2).astype(F32) * (-math.log(10000.0) / 256))
    angle = (starts[0] + ten * 128 + row).astype(F32) * inv_freq
    cos_v[...] = jnp.cos(angle)
    sine = jnp.sin(angle)
    sin_v[...] = jnp.where(even, -sine, sine)

    def rotate(v):
        swap = jnp.where(even, pltpu.roll(v, 255, 1), pltpu.roll(v, 1, 1))
        return v * cos_v[...] + swap * sin_v[...]

    got_wkv.wait()
    keyval = jnp.dot(normed[...], wkv[...], preferred_element_type=F32)
    window[8 + ten, :, 0:256] = rotate(keyval[:, 0:256]).astype(BF16)
    window[8 + ten, :, 256:512] = keyval[:, 256:512].astype(BF16)

    for k in range(1, 8):
        p = (ten + k) % 8

        @pl.when(p > ten)
        def _():
            ref = window.at[8 + ten]
            push(ref, ref, key_send.at[p], key_recv.at[ten], dev(rep, dp, p))

    for i in (0, 1, 2, 3):
        relay(0, i)

    got_pages.wait()
    for k in (-3, -2, -1, 1, 2, 3):
        arrive(near_pages.at[pl.ds((3 - k) * 8, 8)], page_recv.at[3 - k], page_send.at[0])
    arrive(table_in, table_sem.at[1], table_sem.at[0])
    to_scalars = pltpu.make_async_copy(table_in, table_s, local_sem.at[5])
    to_scalars.start()
    to_scalars.wait()

    def place(page):
        step = (page // 8 + (n_dp + 3) - dp) % n_dp
        return jnp.minimum(step, 6) * 8 + page % 8

    for j in range(8):
        theirs[j] = near_pages[place(table_s[0, j])]
    swap_copy = push(theirs, swapped, swap_send.at[0], swap_recv.at[0], twin)
    for j in range(8):
        mine[j] = near_pages[place(page_table[0, j])]
    for i in (4, 5, 6):
        relay(0, i)
    arrive(swapped, swap_recv.at[0], swap_send.at[0])
    for j in range(8):
        slots[j] = jnp.where(page_table[0, j] // (8 * n_dp) == rep, mine[j], swapped[j])

    for k in range(1, 8):
        p = (ten + k) % 8
        for m in range(4):

            @pl.when(2 * m + 1 >= p)
            def _():
                push(
                    slots.at[pl.ds(2 * m, 2)],
                    window.at[pl.ds(2 * m, 2), pl.ds(pl.multiple_of(ten * 16, 16), 16), :],
                    slot_send.at[p, m],
                    slot_recv.at[ten, m],
                    dev(rep, dp, p),
                )

    for j in range(8):
        window[j, pl.ds(pl.multiple_of(ten * 16, 16), 16), :] = slots[j]

    open_(1)
    for i in range(7):
        across(0, i)
    for i in (0, 1, 2, 3):
        relay(1, i)
    for i in range(7):
        settle(0, i)

    for h in range(6):
        q = lax.dot_general(normed[...], wq[256 * h : 256 * h + 256, :], NT, preferred_element_type=F32)
        query[128 * h : 128 * h + 128, :] = rotate(q).astype(BF16)

    for i in (4, 5, 6):
        relay(1, i)

    for k in range(1, 8):
        p = (ten + k) % 8

        @pl.when(p < ten)
        def _():
            arrive(window.at[8 + p], key_recv.at[p], key_send.at[0])

        for m in range(4):

            @pl.when(2 * m + 1 >= ten)
            def _():
                arrive(
                    window.at[pl.ds(2 * m, 2), pl.ds(pl.multiple_of(p * 16, 16), 16), :],
                    slot_recv.at[p, m],
                    slot_send.at[0, 0],
                )

    rows = lax.broadcasted_iota(jnp.int32, (128, 1152), 0)
    keyed = lax.broadcasted_iota(jnp.int32, (128, 1152), 1)
    seen = (keyed >= rows + 1) & (keyed <= rows + 1024)
    for h in range(6):
        keys = window[pl.ds(ten, 9), :, 0:256].reshape(1152, 256)
        scores = lax.dot_general(query[128 * h : 128 * h + 128, :], keys, NT, preferred_element_type=F32)
        scores = jnp.where(seen, scores * (1.0 / 16.0), -1e30)
        top = jnp.max(scores, axis=-1, keepdims=True)
        expd = jnp.exp(scores - top)
        total = jnp.sum(expd, axis=-1, keepdims=True)
        values = window[pl.ds(ten, 9), :, 256:512].reshape(1152, 256)
        got = jnp.dot(expd.astype(BF16), values, preferred_element_type=F32)
        mixed[:, 256 * h : 256 * h + 256] = (got / total).astype(BF16)
        across(1, h)
    across(1, 6)

    for i in range(7):
        settle(1, i)
    acc[...] = jnp.dot(mixed[...], wo[...], preferred_element_type=F32)
    live = ten * 128 + lax.broadcasted_iota(jnp.int32, (128, 1536), 0) < lengths[0]
    out[0] = jnp.where(live, acc[...], 0.0).astype(BF16)

    for copy in sends + page_copies + [table_copy, swap_copy]:
        copy.wait_send()
    for k in range(1, 8):
        p = (ten + k) % 8

        @pl.when(p > ten)
        def _():
            ref = window.at[8 + ten]
            pltpu.make_async_remote_copy(
                src_ref=ref, dst_ref=ref, send_sem=key_send.at[p], recv_sem=key_recv.at[ten],
                device_id=sibling, device_id_type=MESH,
            ).wait_send()

        for m in range(4):

            @pl.when(2 * m + 1 >= p)
            def _():
                ref = slots.at[pl.ds(2 * m, 2)]
                pltpu.make_async_remote_copy(
                    src_ref=ref, dst_ref=ref, send_sem=slot_send.at[p, m], recv_sem=slot_recv.at[ten, m],
                    device_id=sibling, device_id_type=MESH,
                ).wait_send()


def shards(tokens, norm_gain, w_query, w_keyval, w_out, kv_pages, page_table, lengths, starts):
    smem = pl.BlockSpec(memory_space=pltpu.SMEM)
    vmem = pl.BlockSpec(memory_space=pltpu.VMEM)
    hbm = pl.BlockSpec(memory_space=pl.ANY)
    dma = pltpu.SemaphoreType.DMA
    return pl.pallas_call(
        fused,
        name="fused",
        out_shape=jax.ShapeDtypeStruct((1, 128, 1536), BF16),
        in_specs=[smem, smem, smem, hbm, vmem, hbm, hbm, hbm, hbm],
        out_specs=vmem,
        scratch_shapes=[
            pltpu.VMEM((128, 1536), BF16),
            pltpu.VMEM((128, 1536), BF16),
            pltpu.VMEM((1536, 192), BF16),
            pltpu.VMEM((1536, 512), BF16),
            pltpu.VMEM((1536, 1536), BF16),
            pltpu.VMEM((1536, 1536), BF16),
            pltpu.VMEM((56, 16, 512), BF16),
            pltpu.VMEM((8, 16, 512), BF16),
            pltpu.VMEM((8, 16, 512), BF16),
            pltpu.VMEM((8, 16, 512), BF16),
            pltpu.VMEM((8, 16, 512), BF16),
            pltpu.VMEM((16, 128, 512), BF16),
            pltpu.VMEM((128, 256), F32),
            pltpu.VMEM((128, 256), F32),
            pltpu.VMEM((768, 256), BF16),
            pltpu.VMEM((128, 1536), BF16),
            pltpu.VMEM((128, 1536), F32),
            pltpu.VMEM((8, 128), jnp.int32),
            pltpu.VMEM((8, 128), jnp.int32),
            pltpu.SMEM((8, 128), jnp.int32),
            dma((6,)),
            dma((2, 35)),
            dma((2, 8)),
            dma((2, 8, 2)),
            dma((2, 8, 2)),
            dma((6,)),
            dma((7,)),
            dma((1,)),
            dma((1,)),
            dma((2,)),
            dma((8, 4)),
            dma((8, 4)),
            dma((8,)),
            dma((8,)),
        ],
        compiler_params=pltpu.CompilerParams(
            collective_id=0, has_side_effects=True, vmem_limit_bytes=48 << 20
        ),
    )(page_table, lengths, starts, tokens, norm_gain, w_query, w_keyval, w_out, kv_pages)


def solution(mesh):
    placed = (
        P(("rep", "dp"), "tensor", None),
        P(),
        P(None, "tensor"),
        P(),
        P("tensor", None),
        P(("rep", "dp"), "tensor", None),
        P(("rep", "dp"), None),
        P(("rep", "dp")),
        P(("rep", "dp")),
    )
    return jax.shard_map(
        shards,
        mesh=mesh,
        in_specs=placed,
        out_specs=P(("rep", "dp"), "tensor", None),
        check_vma=False,
    )
```

```python
import functools
import math

import jax
import jax.numpy as jnp
from jax import lax
from jax.experimental import pallas as pl
from jax.experimental.pallas import tpu as pltpu
from jax.sharding import PartitionSpec as P

MESH = pl.DeviceIdType.MESH
BF16 = jnp.bfloat16
F32 = jnp.float32
NT = (((1,), (1,)), ((), ()))


def fused(
    page_table, starts, tokens, gain, w_query, w_keyval, w_out, kv_pages,
    out,
    tok_v, normed, wkv, wq, wo, near_pages, mine, theirs, swapped, slots, window,
    cos_v, sin_v, query, mixed, acc, table_out, table_in, table_s,
    local_sem, w_send, w_direct, w_z, w_core, page_send, page_recv, swap_send, swap_recv,
    table_sem, slot_send, slot_recv, key_send, key_recv,
):
    rep = lax.axis_index("rep")
    dp = lax.axis_index("dp")
    ten = lax.axis_index("tensor")
    core = dp % 2
    par = (dp // 2) % 2
    xh = ten // 4
    y = ten % 4
    n_dp = 32

    def dev(r, d, t):
        return {"rep": r, "dp": d, "tensor": t}

    def near(k):
        return xh * 4 + (y + k) % 4

    def far(k):
        return (1 - xh) * 4 + (y + k) % 4

    y1, y3, y2 = (dev(rep, dp, near(k)) for k in (1, 3, 2))
    cross = dev(1 - rep, dp, far(0))
    twin = dev(1 - rep, dp, ten)
    sibling = dev(rep, dp + 1 - 2 * core, ten)
    z_up = dev(rep, (dp + 2) % n_dp, ten)
    z_down = dev(rep, (dp + n_dp - 2) % n_dp, ten)

    sends = []

    def push(src, dst, send, recv, to):
        copy = pltpu.make_async_remote_copy(
            src_ref=src, dst_ref=dst, send_sem=send, recv_sem=recv, device_id=to, device_id_type=MESH
        )
        copy.start()
        return copy

    def arrive(dst, recv, send):
        pltpu.make_async_remote_copy(
            src_ref=dst, dst_ref=dst, send_sem=send, recv_sem=recv, device_id=sibling, device_id_type=MESH
        ).wait_recv()

    def fetch(src, dst, k):
        copy = pltpu.make_async_copy(src, dst, local_sem.at[k])
        copy.start()
        return copy

    own_rows = pl.ds(pl.multiple_of(ten * 192, 64), 192)
    got_tok = fetch(tokens.at[0], tok_v, 1)
    got_wkv = fetch(w_keyval, wkv, 2)
    got_wq = fetch(w_query, wq.at[own_rows], 0)
    got_pages = fetch(kv_pages, near_pages.at[pl.ds(24, 8)], 4)
    got_wo = fetch(w_out, wo.at[own_rows], 3)

    barrier = pltpu.get_barrier_semaphore()
    peers = [y1, y3, y2, dev(rep, dp, far(0))]
    peers += [cross, twin]
    outer = dev(rep, (dp + n_dp + 6 * core - 3) % n_dp, ten)
    peers += [z_up, z_down, outer, sibling]
    for peer in peers:
        pl.semaphore_signal(barrier, inc=1, device_id=peer, device_id_type=MESH)

    lane = lax.broadcasted_iota(jnp.int32, (8, 128), 1)
    table = jnp.zeros((8, 128), jnp.int32)
    for j in range(8):
        table = jnp.where(lane == j, page_table[0, j], table)
    table_out[...] = table

    row = lax.broadcasted_iota(jnp.int32, (128, 256), 0)
    col = lax.broadcasted_iota(jnp.int32, (128, 256), 1)
    even = col % 2 == 0
    inv_freq = jnp.exp((col - col % 2).astype(F32) * (-math.log(10000.0) / 256))
    angle = (starts[0] + ten * 128 + row).astype(F32) * inv_freq
    cos_v[...] = jnp.cos(angle)
    sine = jnp.sin(angle)
    sin_v[...] = jnp.where(even, -sine, sine)
    got_tok.wait()
    x = tok_v[...].astype(F32)
    scale = lax.rsqrt(jnp.mean(x * x, axis=-1, keepdims=True) + 1e-06)
    normed[...] = (x * scale * gain[...]).astype(BF16)
    got_wq.wait()

    pl.semaphore_wait(barrier, len(peers))

    def held(o):
        return near_pages.at[pl.ds(pl.multiple_of((o + 3) * 8, 8), 8)]

    side = 2 * core - 1
    page_copies = [
        push(kv_pages, held(-2), page_send.at[0], page_recv.at[1], z_up),
        push(kv_pages, held(2), page_send.at[1], page_recv.at[5], z_down),
        push(kv_pages, held(-3 * side), page_send.at[2], page_recv.at[3 - 3 * side], outer),
        push(kv_pages, held(side), page_send.at[3], page_recv.at[3 + side], sibling),
    ]
    table_copy = push(table_out, table_in, table_sem.at[0], table_sem.at[1], twin)

    turn = (xh + rep) % 2
    foreign = [
        near(1), near(3), far(0), turn * 4 + (y + 2) % 4, far(1), far(3), (1 - turn) * 4 + (y + 2) % 4
    ]
    mats = (wq, wo)
    quarter = par * 2 + core

    def piece(m, s, q):
        return mats[m].at[pl.ds(pl.multiple_of(s * 192 + q * 48, 16), 48), :]

    def half(m, s, q, h):
        return mats[m].at[pl.ds(pl.multiple_of(s * 192 + q * 48, 16), 48), pl.ds(h * 768, 768)]

    def open_(m):
        ref = piece(m, ten, quarter)
        for i, to in enumerate((y1, y3, cross)):
            sends.append(push(ref, ref, w_send.at[m, i], w_direct.at[m, ten], to))

        @pl.when(rep == 0)
        def _():
            push(ref, ref, w_send.at[m, 3], w_direct.at[m, ten], y2)

    def shut(m):
        ref = piece(m, ten, quarter)
        pltpu.make_async_remote_copy(
            src_ref=ref, dst_ref=ref, send_sem=w_send.at[m, 3], recv_sem=w_direct.at[m, ten],
            device_id=y2, device_id_type=MESH,
        ).wait_send()

    def relay(m, i):
        s = foreign[i]
        ref = piece(m, s, quarter)
        arrive(ref, w_direct.at[m, s], w_send.at[m, 0])
        if i in (0, 1):
            sends.append(push(ref, ref, w_send.at[m, 4 + i], w_direct.at[m, s], cross))
        if i == 2:

            @pl.when(rep == 1)
            def _():
                push(ref, ref, w_send.at[m, 3], w_direct.at[m, s], y2)

        if i == 3:
            sends.append(push(ref, ref, w_send.at[m, 6], w_direct.at[m, s], twin))
        for h, to in ((0, z_up), (1, z_down)):
            part = half(m, s, quarter, h)
            sends.append(push(part, part, w_send.at[m, 7 + 2 * i + h], w_z.at[m, s, h], to))
        sends.append(push(ref, ref, w_send.at[m, 21 + i], w_core.at[m, s, par], sibling))

    def across(m, i):
        s = foreign[i]
        q = (1 - par) * 2 + core
        for h in (0, 1):
            arrive(half(m, s, q, h), w_z.at[m, s, h], w_send.at[m, 0])
        ref = piece(m, s, q)
        sends.append(push(ref, ref, w_send.at[m, 28 + i], w_core.at[m, s, 1 - par], sibling))

    def settle(m, s):
        for k in (0, 1):
            arrive(piece(m, s, k * 2 + 1 - core), w_core.at[m, s, k], w_send.at[m, 0])

    open_(0)

    def rotate(v):
        swap = jnp.where(even, pltpu.roll(v, 255, 1), pltpu.roll(v, 1, 1))
        return v * cos_v[...] + swap * sin_v[...]

    got_wkv.wait()
    keyval = jnp.dot(normed[...], wkv[...], preferred_element_type=F32)
    window[8 + ten, :, 0:256] = rotate(keyval[:, 0:256]).astype(BF16)
    window[8 + ten, :, 256:512] = keyval[:, 256:512].astype(BF16)

    opposite = dev(rep, dp, far(0))

    def key_copy(t, k, to):
        ref = window.at[8 + t]
        return pltpu.make_async_remote_copy(
            src_ref=ref, dst_ref=ref, send_sem=key_send.at[k], recv_sem=key_recv.at[t],
            device_id=to, device_id_type=MESH,
        )

    def new_keys(act):
        @pl.when(xh == 0)
        def _():
            act(key_copy(ten, 0, opposite))

        for k in (1, 2, 3):

            @pl.when(near(k) > ten)
            def _():
                act(key_copy(ten, k, dev(rep, dp, near(k))))

    def far_keys(act):
        for k in (1, 2, 3):
            act(key_copy(far(0), 3 + k, dev(rep, dp, near(k))))

    new_keys(lambda copy: copy.start())

    for i in (0, 1, 2):
        relay(0, i)

    for k, o in ((4, -2), (5, 2)):
        arrive(held(o), page_recv.at[o + 3], page_send.at[0])
        page_copies.append(
            push(held(o), held(o + side), page_send.at[k], page_recv.at[o + 3 + side], sibling)
        )
    got_wo.wait()
    open_(1)

    @pl.when(xh == 1)
    def _():
        arrive(window.at[8 + far(0)], key_recv.at[far(0)], key_send.at[0])
        far_keys(lambda copy: copy.start())

    got_pages.wait()
    arrive(table_in, table_sem.at[1], table_sem.at[0])
    to_scalars = pltpu.make_async_copy(table_in, table_s, local_sem.at[5])
    to_scalars.start()
    to_scalars.wait()
    for o in (-side, 3 * side, -2 - side, 2 - side):
        arrive(held(o), page_recv.at[o + 3], page_send.at[0])

    def place(page):
        step = (page // 8 + (n_dp + 3) - dp) % n_dp
        return jnp.minimum(step, 6) * 8 + page % 8

    for j in range(8):
        theirs[j] = near_pages[place(table_s[0, j])]
    swap_copy = push(theirs, swapped, swap_send.at[0], swap_recv.at[0], twin)
    for j in range(8):
        mine[j] = near_pages[place(page_table[0, j])]
    for i in (3, 4, 5):
        relay(0, i)
    arrive(swapped, swap_recv.at[0], swap_send.at[0])
    for j in range(8):
        slots[j] = jnp.where(page_table[0, j] // (8 * n_dp) == rep, mine[j], swapped[j])

    for j in range(8):
        window[j, pl.ds(pl.multiple_of(ten * 16, 16), 16), :] = slots[j]

    def slot_copy(t, m, k, to):
        ref = window.at[pl.ds(2 * m, 2), pl.ds(pl.multiple_of(t * 16, 16), 16), :]
        return pltpu.make_async_remote_copy(
            src_ref=ref, dst_ref=ref, send_sem=slot_send.at[k, m], recv_sem=slot_recv.at[t, m],
            device_id=to, device_id_type=MESH,
        )

    def own_slots(act):
        for m in (3, 2, 1, 0):

            @pl.when(2 * m + 1 >= 4 - 4 * xh)
            def _():
                act(slot_copy(ten, m, 0, opposite))

        for m in (3, 2, 1, 0):
            for k in (1, 3, 2):

                @pl.when(2 * m + 1 >= near(k))
                def _():
                    act(slot_copy(ten, m, k, dev(rep, dp, near(k))))

    def far_slots(act):
        for m in (3, 2, 1, 0):
            for k in (1, 3, 2):

                @pl.when(2 * m + 1 >= near(k))
                def _():
                    act(slot_copy(far(0), m, 3 + k, dev(rep, dp, near(k))))

    own_slots(lambda copy: copy.start())

    for i in (0, 1, 2):
        relay(1, i)
    relay(0, 6)
    for m in (3, 2, 1, 0):

        @pl.when(2 * m + 1 >= 4 * xh)
        def _():
            arrive(
                window.at[pl.ds(2 * m, 2), pl.ds(pl.multiple_of(far(0) * 16, 16), 16), :],
                slot_recv.at[far(0), m],
                slot_send.at[0, 0],
            )

    far_slots(lambda copy: copy.start())
    for i in (0, 1, 2):
        across(0, i)
    for i in (3, 4, 5):
        relay(1, i)
    for i in (3, 4, 5, 6):
        across(0, i)
    relay(1, 6)
    for s in foreign:
        settle(0, s)

    for h in range(6):
        q = lax.dot_general(normed[...], wq[256 * h : 256 * h + 256, :], NT, preferred_element_type=F32)
        query[128 * h : 128 * h + 128, :] = rotate(q).astype(BF16)

    for i, p in enumerate([near(1), near(3), near(2), far(1), far(3), far(2)]):

        @pl.when(p < ten)
        def _():
            arrive(window.at[8 + p], key_recv.at[p], key_send.at[0])

        for m in range(4):

            @pl.when(2 * m + 1 >= ten)
            def _():
                arrive(
                    window.at[pl.ds(2 * m, 2), pl.ds(pl.multiple_of(p * 16, 16), 16), :],
                    slot_recv.at[p, m],
                    slot_send.at[0, 0],
                )

    rows = lax.broadcasted_iota(jnp.int32, (128, 1152), 0)
    keyed = lax.broadcasted_iota(jnp.int32, (128, 1152), 1)
    seen = (keyed >= rows + 1) & (keyed <= rows + 1024)
    for h in range(6):
        keys = window[pl.ds(ten, 9), :, 0:256].reshape(1152, 256)
        scores = lax.dot_general(query[128 * h : 128 * h + 128, :], keys, NT, preferred_element_type=F32)
        scores = jnp.where(seen, scores * (1.0 / 16.0), -1e30)
        top = jnp.max(scores, axis=-1, keepdims=True)
        expd = jnp.exp(scores - top)
        total = jnp.sum(expd, axis=-1, keepdims=True)
        values = window[pl.ds(ten, 9), :, 256:512].reshape(1152, 256)
        got = jnp.dot(expd.astype(BF16), values, preferred_element_type=F32)
        mixed[:, 256 * h : 256 * h + 256] = (got / total).astype(BF16)
        across(1, h)
    across(1, 6)

    def pair(u):
        cols = mixed[:, pl.ds(pl.multiple_of(u * 384, 384), 384)]
        return jnp.dot(cols, wo[pl.ds(pl.multiple_of(u * 384, 384), 384), :], preferred_element_type=F32)

    for k in (1, 3, 2):
        settle(1, near(k))
    acc[...] = pair(xh * 2)
    acc[...] += pair(xh * 2 + 1)
    for k in range(4):
        settle(1, far(k))
    acc[...] += pair(2 - xh * 2)
    acc[...] += pair(3 - xh * 2)
    out[...] = acc[...].astype(BF16)

    for copy in sends + page_copies + [table_copy, swap_copy]:
        copy.wait_send()
    for m in (0, 1):
        shut(m)
    new_keys(lambda copy: copy.wait_send())

    @pl.when(xh == 1)
    def _():
        far_keys(lambda copy: copy.wait_send())

    own_slots(lambda copy: copy.wait_send())
    far_slots(lambda copy: copy.wait_send())


def shards(tokens, norm_gain, w_query, w_keyval, w_out, kv_pages, page_table, lengths, starts):
    smem = pl.BlockSpec(memory_space=pltpu.SMEM)
    vmem = pl.BlockSpec(memory_space=pltpu.VMEM)
    hbm = pl.BlockSpec(memory_space=pltpu.HBM)
    dma = pltpu.SemaphoreType.DMA
    summed = pl.pallas_call(
        fused,
        name="fused",
        out_shape=jax.ShapeDtypeStruct((128, 1536), BF16),
        in_specs=[smem, smem, hbm, vmem, hbm, hbm, hbm, hbm],
        out_specs=vmem,
        scratch_shapes=[
            pltpu.VMEM((128, 1536), BF16),
            pltpu.VMEM((128, 1536), BF16),
                pltpu.VMEM((1536, 512), BF16),
            pltpu.VMEM((1536, 1536), BF16),
            pltpu.VMEM((1536, 1536), BF16),
            pltpu.VMEM((56, 16, 512), BF16),
            pltpu.VMEM((8, 16, 512), BF16),
            pltpu.VMEM((8, 16, 512), BF16),
            pltpu.VMEM((8, 16, 512), BF16),
            pltpu.VMEM((8, 16, 512), BF16),
            pltpu.VMEM((16, 128, 512), BF16),
            pltpu.VMEM((128, 256), F32),
            pltpu.VMEM((128, 256), F32),
            pltpu.VMEM((768, 256), BF16),
            pltpu.VMEM((128, 1536), BF16),
            pltpu.VMEM((128, 1536), F32),
            pltpu.VMEM((8, 128), jnp.int32),
            pltpu.VMEM((8, 128), jnp.int32),
            pltpu.SMEM((8, 128), jnp.int32),
            dma((6,)),
            dma((2, 35)),
            dma((2, 8)),
            dma((2, 8, 2)),
            dma((2, 8, 2)),
            dma((6,)),
            dma((7,)),
            dma((1,)),
            dma((1,)),
            dma((2,)),
            dma((8, 4)),
            dma((8, 4)),
            dma((8,)),
            dma((8,)),
        ],
        compiler_params=pltpu.CompilerParams(
            collective_id=0, has_side_effects=True, vmem_limit_bytes=61 << 20
        ),
    )(page_table, starts, tokens, norm_gain, w_query.T, w_keyval, w_out, kv_pages)
    live = lax.axis_index("tensor") * 128 + jnp.arange(128, dtype=jnp.int32) < lengths[0]
    return jnp.where(live[:, None], summed, 0)[None]


def solution(mesh):
    placed = (
        P(("rep", "dp"), "tensor", None),
        P(),
        P(None, "tensor"),
        P(),
        P("tensor", None),
        P(("rep", "dp"), "tensor", None),
        P(("rep", "dp"), None),
        P(("rep", "dp")),
        P(("rep", "dp")),
    )
    return jax.shard_map(
        shards,
        mesh=mesh,
        in_specs=placed,
        out_specs=P(("rep", "dp"), "tensor", None),
        check_vma=False,
    )
```

```python
import functools
import math

import jax
import jax.numpy as jnp
from jax import lax
from jax.experimental import pallas as pl
from jax.experimental.pallas import tpu as pltpu
from jax.sharding import PartitionSpec as P

MESH = pl.DeviceIdType.MESH
BF16 = jnp.bfloat16
F32 = jnp.float32
NT = (((1,), (1,)), ((), ()))


TWIN = False
BOTH = False
ORDER = (('begin', 0), ('new',), ('relay', 0, 0), ('relay', 0, 1), ('relay', 0, 2), ('share',), ('begin', 1), ('swap',), ('far',), ('relay', 0, 3), ('relay', 0, 4), ('relay', 0, 5), ('slots',), ('relay', 1, 0), ('relay', 1, 1), ('relay', 1, 2), ('relay', 0, 6), ('pass',), ('across', 0, 0), ('across', 0, 1), ('across', 0, 2), ('relay', 1, 3), ('relay', 1, 4), ('relay', 1, 5), ('across', 0, 3), ('across', 0, 4), ('across', 0, 5), ('across', 0, 6), ('relay', 1, 6), ('across', 1, 0), ('across', 1, 1), ('project', 0), ('project', 1), ('across', 1, 2), ('across', 1, 3), ('across', 1, 4), ('here',), ('attend', 0), ('across', 1, 5), ('across', 1, 6), ('attend', 1), ('finish', 0), ('finish', 1))


def fused(
    page_table, starts, tokens, gain, w_query, w_keyval, w_out, kv_pages,
    out,
    tok_v, normed, wkv, wq, wo, near_pages, mine, theirs, swapped, slots, window,
    cos_v, sin_v, query, mixed, acc, table_out, table_in, table_s,
    local_sem, w_send, w_direct, w_z, w_core, page_send, page_recv, swap_send, swap_recv,
    table_sem, slot_send, slot_recv, key_send, key_recv,
):
    rep = lax.axis_index("rep")
    dp = lax.axis_index("dp")
    ten = lax.axis_index("tensor")
    core = dp % 2
    par = (dp // 2) % 2
    xh = ten // 4
    y = ten % 4
    n_dp = 32

    def dev(r, d, t):
        return {"rep": r, "dp": d, "tensor": t}

    def near(k):
        return xh * 4 + (y + k) % 4

    def far(k):
        return (1 - xh) * 4 + (y + k) % 4

    y1, y3, y2 = (dev(rep, dp, near(k)) for k in (1, 3, 2))
    cross = dev(1 - rep, dp, far(0))
    twin = dev(1 - rep, dp, ten)
    sibling = dev(rep, dp + 1 - 2 * core, ten)
    z_up = dev(rep, (dp + 2) % n_dp, ten)
    z_down = dev(rep, (dp + n_dp - 2) % n_dp, ten)

    sends = []

    def push(src, dst, send, recv, to):
        copy = pltpu.make_async_remote_copy(
            src_ref=src, dst_ref=dst, send_sem=send, recv_sem=recv, device_id=to, device_id_type=MESH
        )
        copy.start()
        return copy

    def arrive(dst, recv, send):
        pltpu.make_async_remote_copy(
            src_ref=dst, dst_ref=dst, send_sem=send, recv_sem=recv, device_id=sibling, device_id_type=MESH
        ).wait_recv()

    def fetch(src, dst, k):
        copy = pltpu.make_async_copy(src, dst, local_sem.at[k])
        copy.start()
        return copy

    own_rows = pl.ds(pl.multiple_of(ten * 192, 64), 192)
    got_tok = fetch(tokens.at[0], tok_v, 1)
    got_wkv = fetch(w_keyval, wkv, 2)
    got_wq = fetch(w_query, wq.at[own_rows], 0)
    got_pages = fetch(kv_pages, near_pages.at[pl.ds(24, 8)], 4)
    got_wo = fetch(w_out, wo.at[own_rows], 3)

    barrier = pltpu.get_barrier_semaphore()
    peers = [y1, y3, y2, dev(rep, dp, far(0))]
    peers += [cross, twin]
    outer = dev(rep, (dp + n_dp + 6 * core - 3) % n_dp, ten)
    peers += [z_up, z_down, outer, sibling]
    for peer in peers:
        pl.semaphore_signal(barrier, inc=1, device_id=peer, device_id_type=MESH)

    lane = lax.broadcasted_iota(jnp.int32, (8, 128), 1)
    table = jnp.zeros((8, 128), jnp.int32)
    for j in range(8):
        table = jnp.where(lane == j, page_table[0, j], table)
    table_out[...] = table

    row = lax.broadcasted_iota(jnp.int32, (128, 256), 0)
    col = lax.broadcasted_iota(jnp.int32, (128, 256), 1)
    even = col % 2 == 0
    inv_freq = jnp.exp((col - col % 2).astype(F32) * (-math.log(10000.0) / 256))
    angle = (starts[0] + ten * 128 + row).astype(F32) * inv_freq
    cos_v[...] = jnp.cos(angle)
    sine = jnp.sin(angle)
    sin_v[...] = jnp.where(even, -sine, sine)
    got_tok.wait()
    x = tok_v[...].astype(F32)
    scale = lax.rsqrt(jnp.mean(x * x, axis=-1, keepdims=True) + 1e-06)
    normed[...] = (x * scale * gain[...]).astype(BF16)
    got_wq.wait()

    pl.semaphore_wait(barrier, len(peers))

    def held(o):
        return near_pages.at[pl.ds(pl.multiple_of((o + 3) * 8, 8), 8)]

    side = 2 * core - 1
    page_copies = [
        push(kv_pages, held(-2), page_send.at[0], page_recv.at[1], z_up),
        push(kv_pages, held(2), page_send.at[1], page_recv.at[5], z_down),
        push(kv_pages, held(-3 * side), page_send.at[2], page_recv.at[3 - 3 * side], outer),
        push(kv_pages, held(side), page_send.at[3], page_recv.at[3 + side], sibling),
    ]
    table_copy = push(table_out, table_in, table_sem.at[0], table_sem.at[1], twin)

    turn = (xh + rep) % 2
    foreign = [
        near(1), near(3), far(0), turn * 4 + (y + 2) % 4,
        far(3 - 2 * rep) if TWIN else far(1), far(1 + 2 * rep) if TWIN else far(3),
        (1 - turn) * 4 + (y + 2) % 4,
    ]
    mats = (wq, wo)
    quarter = par * 2 + core

    def piece(m, s, q):
        return mats[m].at[pl.ds(pl.multiple_of(s * 192 + q * 48, 16), 48), :]

    def half(m, s, q, h):
        return mats[m].at[pl.ds(pl.multiple_of(s * 192 + q * 48, 16), 48), pl.ds(h * 768, 768)]

    def open_(m):
        ref = piece(m, ten, quarter)
        for i, to in enumerate((y1, y3, cross)):
            sends.append(push(ref, ref, w_send.at[m, i], w_direct.at[m, ten], to))

        @pl.when(rep == 0)
        def _():
            push(ref, ref, w_send.at[m, 3], w_direct.at[m, ten], y2)

        if BOTH:
            ref = piece(m, ten, (1 - par) * 2 + core)
            sends.append(push(ref, ref, w_send.at[m, 6], w_z.at[m, ten, 0], cross))

    def shut(m):
        ref = piece(m, ten, quarter)
        for k in (3, 4) if TWIN else (3,):
            pltpu.make_async_remote_copy(
                src_ref=ref, dst_ref=ref, send_sem=w_send.at[m, k], recv_sem=w_direct.at[m, ten],
                device_id=y2, device_id_type=MESH,
            ).wait_send()

    def relay(m, i):
        s = foreign[i]
        ref = piece(m, s, quarter)
        arrive(ref, w_direct.at[m, s], w_send.at[m, 0])
        if i in (0, 1):
            if TWIN:

                @pl.when(rep == i)
                def _():
                    push(ref, ref, w_send.at[m, 4], w_direct.at[m, s], cross)

            else:
                sends.append(push(ref, ref, w_send.at[m, 4 + i], w_direct.at[m, s], cross))
        if i == 2:

            @pl.when(rep == 1)
            def _():
                push(ref, ref, w_send.at[m, 3], w_direct.at[m, s], y2)

        if i == 3 or (TWIN and i == 4):
            sends.append(push(ref, ref, w_send.at[m, 5 if i == 4 else 35], w_direct.at[m, s], twin))
        for h, to in () if BOTH and i == 2 else ((0, z_up), (1, z_down)):
            part = half(m, s, quarter, h)
            sends.append(push(part, part, w_send.at[m, 7 + 2 * i + h], w_z.at[m, s, h], to))
        sends.append(push(ref, ref, w_send.at[m, 21 + i], w_core.at[m, s, par], sibling))

    def across(m, i):
        s = foreign[i]
        q = (1 - par) * 2 + core
        ref = piece(m, s, q)
        if BOTH and i == 2:
            arrive(ref, w_z.at[m, s, 0], w_send.at[m, 0])
        else:
            for h in (0, 1):
                arrive(half(m, s, q, h), w_z.at[m, s, h], w_send.at[m, 0])
        sends.append(push(ref, ref, w_send.at[m, 28 + i], w_core.at[m, s, 1 - par], sibling))

    def settle(m, s):
        for k in (0, 1):
            arrive(piece(m, s, k * 2 + 1 - core), w_core.at[m, s, k], w_send.at[m, 0])

    def rotate(v):
        swap = jnp.where(even, pltpu.roll(v, 255, 1), pltpu.roll(v, 1, 1))
        return v * cos_v[...] + swap * sin_v[...]

    opposite = dev(rep, dp, far(0))

    def key_copy(t, k, to):
        ref = window.at[8 + t]
        return pltpu.make_async_remote_copy(
            src_ref=ref, dst_ref=ref, send_sem=key_send.at[k], recv_sem=key_recv.at[t],
            device_id=to, device_id_type=MESH,
        )

    def new_keys(act):
        @pl.when(xh == 0)
        def _():
            act(key_copy(ten, 0, opposite))

        for k in (1, 2, 3):

            @pl.when(near(k) > ten)
            def _():
                act(key_copy(ten, k, dev(rep, dp, near(k))))

    def far_keys(act):
        for k in (1, 2, 3):
            act(key_copy(far(0), 3 + k, dev(rep, dp, near(k))))

    def slot_copy(t, m, k, to):
        ref = window.at[pl.ds(2 * m, 2), pl.ds(pl.multiple_of(t * 16, 16), 16), :]
        return pltpu.make_async_remote_copy(
            src_ref=ref, dst_ref=ref, send_sem=slot_send.at[k, m], recv_sem=slot_recv.at[t, m],
            device_id=to, device_id_type=MESH,
        )

    def own_slots(act):
        for m in (3, 2, 1, 0):

            @pl.when(2 * m + 1 >= 4 - 4 * xh)
            def _():
                act(slot_copy(ten, m, 0, opposite))

        for m in (3, 2, 1, 0):
            for k in (1, 3, 2):

                @pl.when(2 * m + 1 >= near(k))
                def _():
                    act(slot_copy(ten, m, k, dev(rep, dp, near(k))))

    def far_slots(act):
        for m in (3, 2, 1, 0):
            for k in (1, 3, 2):

                @pl.when(2 * m + 1 >= near(k))
                def _():
                    act(slot_copy(far(0), m, 3 + k, dev(rep, dp, near(k))))

    def place(page):
        step = (page // 8 + (n_dp + 3) - dp) % n_dp
        return jnp.minimum(step, 6) * 8 + page % 8

    def pair(u):
        cols = mixed[:, pl.ds(pl.multiple_of(u * 384, 384), 384)]
        return jnp.dot(cols, wo[pl.ds(pl.multiple_of(u * 384, 384), 384), :], preferred_element_type=F32)

    def new_block():
        got_wkv.wait()
        keyval = jnp.dot(normed[...], wkv[...], preferred_element_type=F32)
        window[8 + ten, :, 0:256] = rotate(keyval[:, 0:256]).astype(BF16)
        window[8 + ten, :, 256:512] = keyval[:, 256:512].astype(BF16)

        new_keys(lambda copy: copy.start())

    def far_block():
        @pl.when(xh == 1)
        def _():
            arrive(window.at[8 + far(0)], key_recv.at[far(0)], key_send.at[0])
            far_keys(lambda copy: copy.start())

    def share_pages():
        for k, o in ((4, -2), (5, 2)):
            arrive(held(o), page_recv.at[o + 3], page_send.at[0])
            page_copies.append(
                push(held(o), held(o + side), page_send.at[k], page_recv.at[o + 3 + side], sibling)
            )

    def swap_pages():
        got_pages.wait()
        arrive(table_in, table_sem.at[1], table_sem.at[0])
        to_scalars = pltpu.make_async_copy(table_in, table_s, local_sem.at[5])
        to_scalars.start()
        to_scalars.wait()
        for o in (-side, 3 * side, -2 - side, 2 - side):
            arrive(held(o), page_recv.at[o + 3], page_send.at[0])

        for j in range(8):
            theirs[j] = near_pages[place(table_s[0, j])]
        push(theirs, swapped, swap_send.at[0], swap_recv.at[0], twin)
        for j in range(8):
            mine[j] = near_pages[place(page_table[0, j])]

    def send_slots():
        arrive(swapped, swap_recv.at[0], swap_send.at[0])
        for j in range(8):
            slots[j] = jnp.where(page_table[0, j] // (8 * n_dp) == rep, mine[j], swapped[j])

        for j in range(8):
            window[j, pl.ds(pl.multiple_of(ten * 16, 16), 16), :] = slots[j]

        own_slots(lambda copy: copy.start())

    def pass_slots():
        for m in (3, 2, 1, 0):

            @pl.when(2 * m + 1 >= 4 * xh)
            def _():
                arrive(
                    window.at[pl.ds(2 * m, 2), pl.ds(pl.multiple_of(far(0) * 16, 16), 16), :],
                    slot_recv.at[far(0), m],
                    slot_send.at[0, 0],
                )

        far_slots(lambda copy: copy.start())

    def all_here():
        for i, p in enumerate([near(1), near(3), near(2), far(1), far(3), far(2)]):

            @pl.when(p < ten)
            def _():
                arrive(window.at[8 + p], key_recv.at[p], key_send.at[0])

            for m in range(4):

                @pl.when(2 * m + 1 >= ten)
                def _():
                    arrive(
                        window.at[pl.ds(2 * m, 2), pl.ds(pl.multiple_of(p * 16, 16), 16), :],
                        slot_recv.at[p, m],
                        slot_send.at[0, 0],
                    )

    def project(k):
        side_of = (xh + k) % 2
        for i in range(1 - k, 4):
            settle(0, side_of * 4 + (y + i) % 4)
        for i in range(3):
            h = side_of * 3 + i
            q = lax.dot_general(
                normed[...], wq[pl.ds(pl.multiple_of(256 * h, 256), 256), :], NT, preferred_element_type=F32
            )
            query[pl.ds(pl.multiple_of(128 * h, 128), 128), :] = rotate(q).astype(BF16)

    def attend(k):
        first = 3 * ((xh + k) % 2)
        part = pl.ds(pl.multiple_of(128 * first, 128), 384)
        keys = window[pl.ds(ten, 9), :, 0:256].reshape(1152, 256)
        scores = lax.dot_general(query[part, :], keys, NT, preferred_element_type=F32) * (1.0 / 16.0)
        rows = lax.broadcasted_iota(jnp.int32, (384, 128), 0) % 128
        lanes = lax.broadcasted_iota(jnp.int32, (384, 128), 1)
        scores = jnp.concatenate(
            [
                jnp.where(lanes >= rows + 1, scores[:, :128], -1e30),
                scores[:, 128:1024],
                jnp.where(lanes <= rows, scores[:, 1024:], -1e30),
            ],
            axis=1,
        )
        top = jnp.max(scores, axis=-1, keepdims=True)
        expd = jnp.exp(scores - top)
        total = jnp.sum(expd, axis=-1, keepdims=True)
        values = window[pl.ds(ten, 9), :, 256:512].reshape(1152, 256)
        got = jnp.dot(expd.astype(BF16), values, preferred_element_type=F32)
        got = (got / total).astype(BF16)
        for i in range(3):
            mixed[:, pl.ds(pl.multiple_of(256 * (first + i), 256), 256)] = got[128 * i : 128 * i + 128]

    def finish(k):
        side_of = (xh + k) % 2
        for i in range(1 - k, 4):
            settle(1, side_of * 4 + (y + i) % 4)
        if k == 0:
            acc[...] = pair(side_of * 2)
        else:
            acc[...] += pair(side_of * 2)
        acc[...] += pair(side_of * 2 + 1)

    def begin(m):
        if m == 1:
            got_wo.wait()
        open_(m)

    steps = {
        "begin": begin, "relay": relay, "across": across, "new": new_block, "far": far_block,
        "share": share_pages, "swap": swap_pages, "slots": send_slots, "pass": pass_slots, "here": all_here,
        "project": project, "attend": attend, "finish": finish,
    }
    for step in ORDER:
        steps[step[0]](*step[1:])

    out[...] = acc[...].astype(BF16)

    for copy in sends + page_copies + [table_copy]:
        copy.wait_send()
    pltpu.make_async_remote_copy(
        src_ref=theirs, dst_ref=swapped, send_sem=swap_send.at[0], recv_sem=swap_recv.at[0],
        device_id=twin, device_id_type=MESH,
    ).wait_send()
    for m in (0, 1):
        shut(m)
    new_keys(lambda copy: copy.wait_send())

    @pl.when(xh == 1)
    def _():
        far_keys(lambda copy: copy.wait_send())

    own_slots(lambda copy: copy.wait_send())
    far_slots(lambda copy: copy.wait_send())


def shards(tokens, norm_gain, w_query, w_keyval, w_out, kv_pages, page_table, lengths, starts):
    smem = pl.BlockSpec(memory_space=pltpu.SMEM)
    vmem = pl.BlockSpec(memory_space=pltpu.VMEM)
    hbm = pl.BlockSpec(memory_space=pltpu.HBM)
    dma = pltpu.SemaphoreType.DMA
    summed = pl.pallas_call(
        fused,
        name="fused",
        out_shape=jax.ShapeDtypeStruct((128, 1536), BF16),
        in_specs=[smem, smem, hbm, vmem, hbm, hbm, hbm, hbm],
        out_specs=vmem,
        scratch_shapes=[
            pltpu.VMEM((128, 1536), BF16),
            pltpu.VMEM((128, 1536), BF16),
                pltpu.VMEM((1536, 512), BF16),
            pltpu.VMEM((1536, 1536), BF16),
            pltpu.VMEM((1536, 1536), BF16),
            pltpu.VMEM((56, 16, 512), BF16),
            pltpu.VMEM((8, 16, 512), BF16),
            pltpu.VMEM((8, 16, 512), BF16),
            pltpu.VMEM((8, 16, 512), BF16),
            pltpu.VMEM((8, 16, 512), BF16),
            pltpu.VMEM((16, 128, 512), BF16),
            pltpu.VMEM((128, 256), F32),
            pltpu.VMEM((128, 256), F32),
            pltpu.VMEM((768, 256), BF16),
            pltpu.VMEM((128, 1536), BF16),
            pltpu.VMEM((128, 1536), F32),
            pltpu.VMEM((8, 128), jnp.int32),
            pltpu.VMEM((8, 128), jnp.int32),
            pltpu.SMEM((8, 128), jnp.int32),
            dma((6,)),
            dma((2, 36)),
            dma((2, 8)),
            dma((2, 8, 2)),
            dma((2, 8, 2)),
            dma((6,)),
            dma((7,)),
            dma((1,)),
            dma((1,)),
            dma((2,)),
            dma((8, 4)),
            dma((8, 4)),
            dma((8,)),
            dma((8,)),
        ],
        compiler_params=pltpu.CompilerParams(
            collective_id=0, has_side_effects=True, vmem_limit_bytes=61 << 20
        ),
    )(page_table, starts, tokens, norm_gain, w_query.T, w_keyval, w_out, kv_pages)
    live = lax.axis_index("tensor") * 128 + jnp.arange(128, dtype=jnp.int32) < lengths[0]
    return jnp.where(live[:, None], summed, 0)[None]


def solution(mesh):
    placed = (
        P(("rep", "dp"), "tensor", None),
        P(),
        P(None, "tensor"),
        P(),
        P("tensor", None),
        P(("rep", "dp"), "tensor", None),
        P(("rep", "dp"), None),
        P(("rep", "dp")),
        P(("rep", "dp")),
    )
    return jax.shard_map(
        shards,
        mesh=mesh,
        in_specs=placed,
        out_specs=P(("rep", "dp"), "tensor", None),
        check_vma=False,
    )
```
